32 devices in a mesh: slab: 4 (over x, core), trace: 8 (over z, y).
Axes of the slice: x: 2, y: 2, z: 4, core: 2. Of those that a mesh axis runs over, the one named last changes fastest.
Arguments:
- incident: float32 [4, 3072, 128], P(None, 'trace'), may hold values from -6 to 6
- green_interior: bfloat16 [4, 2, 4608, 3072], P('slab', None, 'trace'), may hold values from -0.078125 to 0.078125
- green_next: bfloat16 [4, 2, 3072, 3072], P('slab', None, 'trace'), may hold values from -0.0625 to 0.0625
- sources: float32 [4, 4, 3072, 128], P('slab', None, 'trace'), may hold values from -3 to 3
Outputs:
- interior: float32 [4, 4, 4608, 128], P('slab', None, 'trace')
- traces: float32 [4, 4, 3072, 128], P('slab', None, 'trace')
The draws below stay inside these ranges and needn't reach their ends.
All inputs are finite; a program needn't handle non-finite values.
Results may differ from the reference program's by a relative error of at most 0.014.
Values may be sent and summed in bfloat16 or wider, within the bound.
A program may use at most 64 MiB of HBM per device.

```python
import jax
import jax.numpy as jnp

TR = 3072
INTER = 4608
SRC = 64
FRONTS = 4
SLABS = 4
N_SLAB = 4


def shard_levels(stream_key, extent, cuts, smallest, largest):
    def one(axis_at, blocks):
        heights = jax.random.uniform(jax.random.fold_in(jax.random.fold_in(stream_key, 6), axis_at), (blocks,), jnp.float32, smallest / len(cuts), largest / len(cuts))
        return jnp.repeat(jnp.exp(heights), extent[axis_at] // blocks).reshape((-1,) + (1,) * (len(extent) - axis_at - 1))

    level = one(*cuts[0])
    for cut in cuts[1:]:
        level = level * one(*cut)
    return level


def noise(key, dims, scale, bound, shards=(), kind=jnp.bfloat16):
    factor_of = shard_levels(key, dims, shards, -0.22, 0.18) if shards else 1.0
    result = jax.random.normal(key, dims, jnp.float32) * scale * factor_of
    return jnp.minimum(jnp.maximum(result, -bound), bound).astype(kind)


def setup_inputs(seed: int = 0) -> dict:
    key_of = jax.random.split(jax.random.key(seed), 5)
    return {
        "incident": noise(key_of[0], (FRONTS, TR, 2 * SRC), 1.0, 6.0, ((1, 8),), jnp.float32),
        "green_interior": noise(key_of[1], (SLABS, 2, INTER, TR), (2 * TR) ** -0.5, 0.078125, ((0, 4), (2, 8))),
        "green_next": noise(key_of[2], (SLABS, 2, TR, TR), (5 * TR // 2) ** -0.5, 0.0625, ((0, 4), (2, 8))),
        "sources": noise(key_of[3], (SLABS, FRONTS, TR, 2 * SRC), 0.5, 3.0, ((0, 4), (2, 8)), jnp.float32),
    }


def complex_apply(halves, vectors, batches):
    row_count = halves.shape[1]
    inner_width = halves.shape[2]
    half_cols = vectors.shape[1] // (2 * batches)
    product = jnp.dot(halves.reshape(2 * row_count, inner_width), vectors, preferred_element_type=jnp.float32)
    product = product.reshape(2, row_count, batches, 2, half_cols)
    real_part = product[0, :, :, 0] - product[1, :, :, 1]
    imag_part = product[0, :, :, 1] + product[1, :, :, 0]
    return jnp.stack([real_part, imag_part], axis=2)


def to_fronts(product):
    row_count, batches, two_parts, half_cols = product.shape
    return jnp.transpose(product, (1, 0, 2, 3)).reshape(batches, row_count, two_parts * half_cols)


def reference(incident, green_interior, green_next, sources):
    current = jnp.transpose(incident, (1, 0, 2)).reshape(TR, FRONTS * 2 * SRC).astype(jnp.bfloat16)
    interiors = []
    outgoing = []
    for slab_index in range(N_SLAB):
        interiors.append(to_fronts(complex_apply(green_interior[slab_index], current, FRONTS)))
        leaving = to_fronts(complex_apply(green_next[slab_index], current, FRONTS)) + sources[slab_index]
        outgoing.append(leaving)
        current = jnp.transpose(leaving, (1, 0, 2)).reshape(TR, FRONTS * 2 * SRC).astype(jnp.bfloat16)
    return jnp.stack(interiors), jnp.stack(outgoing)
```

```python
import functools

import jax
import jax.numpy as jnp
from jax import lax
from jax.experimental import pallas as pl
from jax.experimental.pallas import tpu as pltpu
from jax.sharding import PartitionSpec as P

MESH = pl.DeviceIdType.MESH
INNER = 2


def chunk_count(blocks, rows):
    count = 4
    while count > 1 and (blocks % (count * INNER) or (blocks // count * rows) % 128):
        count //= 2
    return count


def combine(first, second):
    lane = lax.broadcasted_iota(jnp.int32, first.shape, 1)
    half = first.shape[1] // 2
    turned = pltpu.roll(second, half, 1)
    return first + jnp.where(lane < half, -turned, turned)


def kernel(
    slabs,
    blocks,
    incident,
    green_interior,
    green_next,
    sources,
    interior,
    traces,
    entering,
    leaving,
    next_op,
    inner_op,
    incoming,
    own_sources,
    next_sum,
    inner_sum,
    trace_out,
    inner_out,
    recv_sem,
    direct_sem,
    relay_sem,
    load_sem,
    store_sem,
):
    fronts, _, rows, columns = entering.shape
    inner_rows = inner_op.shape[1]
    depth = next_op.shape[2]
    outer = blocks // INNER
    chunks = chunk_count(blocks, rows)
    per_chunk = blocks // chunks
    width = depth // chunks
    slab = lax.axis_index("slab")
    me = lax.axis_index("trace")
    lane_pos = lax.rem(me, INNER)
    my_outer = me // INNER
    partner = me + 1 - 2 * lane_pos
    first_slab = slab == 0
    last_slab = slab == slabs - 1
    my_chunk = me // per_chunk

    load_incident = pltpu.make_async_copy(incident, incoming, load_sem.at[0])
    load_next = pltpu.make_async_copy(green_next.at[0], next_op, load_sem.at[1])
    load_sources = pltpu.make_async_copy(sources.at[0], own_sources, load_sem.at[2])
    load_inner = pltpu.make_async_copy(green_interior.at[0], inner_op, load_sem.at[3])

    @pl.when(first_slab)
    def _():
        load_incident.start()

    load_next.start()
    load_sources.start()
    load_inner.start()

    barrier = pltpu.get_barrier_semaphore()

    def greet(target_slab, target):
        pl.semaphore_signal(
            barrier, inc=1, device_id={"slab": target_slab, "trace": target}, device_id_type=MESH
        )

    greet(slab, partner)

    @pl.when(first_slab)
    def _():
        for step in range(1, outer):
            greet(slab, lax.rem(my_outer + step, outer) * INNER + lane_pos)

    @pl.when(jnp.logical_not(first_slab))
    def _():
        for step in range(outer):
            greet(slab - 1, lax.rem(my_outer + step, outer) * INNER + lane_pos)

    peers = jnp.where(first_slab, outer, 1) + jnp.where(last_slab, 0, outer)
    pl.semaphore_wait(barrier, peers)

    def first_copy(front, step):
        target = lax.rem(my_outer + step, outer) * INNER + lane_pos
        return pltpu.make_async_remote_copy(
            src_ref=entering.at[front, me],
            dst_ref=entering.at[front, me],
            send_sem=direct_sem.at[1, front, step],
            recv_sem=recv_sem.at[front, me],
            device_id={"slab": slab, "trace": target},
            device_id_type=MESH,
        )

    def next_copy(front, step):
        target = lax.rem(my_outer + step, outer) * INNER + lane_pos
        return pltpu.make_async_remote_copy(
            src_ref=leaving.at[front],
            dst_ref=entering.at[front, me],
            send_sem=direct_sem.at[0, front, step],
            recv_sem=recv_sem.at[front, me],
            device_id={"slab": slab + 1, "trace": target},
            device_id_type=MESH,
        )

    def relay_copy(front, block):
        return pltpu.make_async_remote_copy(
            src_ref=entering.at[front, block],
            dst_ref=entering.at[front, block],
            send_sem=relay_sem.at[front, block // INNER],
            recv_sem=recv_sem.at[front, block],
            device_id={"slab": slab, "trace": partner},
            device_id_type=MESH,
        )

    def store_trace(front):
        return pltpu.make_async_copy(
            trace_out.at[front], traces.at[0, front], store_sem.at[0, front]
        )

    def store_inner(front):
        return pltpu.make_async_copy(
            inner_out.at[front], interior.at[0, front], store_sem.at[1, front]
        )

    @pl.when(first_slab)
    def _():
        load_incident.wait()
        for front in range(fronts):
            entering[front, me] = incoming[front].astype(jnp.bfloat16)
        for step in range(1, outer):
            first_copy(0, step).start()

    def chunk_at(order):
        return lax.rem(my_chunk + order, chunks)

    def vectors(front, chunk):
        return entering[front, pl.ds(chunk * per_chunk, per_chunk)].reshape(width, columns)

    def add_chunk(op, total, front, chunk, fresh):
        start = pl.multiple_of(chunk * width, width)
        halves = op.shape[1]
        matrix = op[:, :, pl.ds(start, width)].reshape(2 * halves, width)
        product = jnp.dot(
            matrix, vectors(front, chunk), preferred_element_type=jnp.float32
        )
        if fresh:
            total[...] = product
        else:
            total[...] += product

    def inner_chunk(front, order):
        add_chunk(inner_op, inner_sum, front, chunk_at(order), order == 0)
        if order == chunks - 1:
            inner_out[front] = combine(inner_sum[0:inner_rows], inner_sum[inner_rows:])
            store_inner(front).start()

    def one_front(front, carry):
        @pl.when(first_slab & (front + 1 < fronts))
        def _():
            for step in range(1, outer):
                first_copy(front + 1, step).start()

        for order in range(chunks):
            for index in range(per_chunk // INNER):
                block = chunk_at(order) * per_chunk + index * INNER + lane_pos

                @pl.when(jnp.logical_not(first_slab & (block == me)))
                def _():
                    relay_copy(front, block).wait_recv()

                relay_copy(front, block).start()

            @pl.when(front > 0)
            def _():
                inner_chunk(front - 1, order)

        @pl.when(front == 0)
        def _():
            load_next.wait()
            load_sources.wait()
            load_inner.wait()

        for order in range(chunks):
            for index in range(per_chunk // INNER):
                block = chunk_at(order) * per_chunk + index * INNER + 1 - lane_pos
                relay_copy(front, block).wait_recv()
            add_chunk(next_op, next_sum, front, chunk_at(order), order == 0)

        result = combine(next_sum[0:rows], next_sum[rows:]) + own_sources[front]
        trace_out[front] = result
        leaving[front] = result.astype(jnp.bfloat16)

        @pl.when(jnp.logical_not(last_slab))
        def _():
            for step in range(outer):
                next_copy(front, step).start()

        store_trace(front).start()
        return carry

    lax.fori_loop(0, fronts, one_front, 0)
    for order in range(chunks):
        inner_chunk(fronts - 1, order)

    def drain(front, carry):
        @pl.when(first_slab)
        def _():
            for step in range(1, outer):
                first_copy(front, step).wait_send()

        @pl.when(jnp.logical_not(last_slab))
        def _():
            for step in range(outer):
                next_copy(front, step).wait_send()

        for index in range(outer):
            relay_copy(front, index * INNER + lane_pos).wait_send()
        store_trace(front).wait()
        store_inner(front).wait()
        return carry

    lax.fori_loop(0, fronts, drain, 0)


def local(slabs, blocks, incident, green_interior, green_next, sources):
    fronts, rows, columns = incident.shape
    inner_rows = green_interior.shape[2]
    depth = green_next.shape[3]
    outer = blocks // INNER
    anywhere = pl.BlockSpec(memory_space=pl.ANY)
    return pl.pallas_call(
        functools.partial(kernel, slabs, blocks),
        out_shape=(
            jax.ShapeDtypeStruct((1, fronts, inner_rows, columns), jnp.float32),
            jax.ShapeDtypeStruct((1, fronts, rows, columns), jnp.float32),
        ),
        in_specs=[anywhere] * 4,
        out_specs=(anywhere, anywhere),
        scratch_shapes=[
            pltpu.VMEM((fronts, blocks, rows, columns), jnp.bfloat16),
            pltpu.VMEM((fronts, rows, columns), jnp.bfloat16),
            pltpu.VMEM((2, rows, depth), jnp.bfloat16),
            pltpu.VMEM((2, inner_rows, depth), jnp.bfloat16),
            pltpu.VMEM((fronts, rows, columns), jnp.float32),
            pltpu.VMEM((fronts, rows, columns), jnp.float32),
            pltpu.VMEM((2 * rows, columns), jnp.float32),
            pltpu.VMEM((2 * inner_rows, columns), jnp.float32),
            pltpu.VMEM((fronts, rows, columns), jnp.float32),
            pltpu.VMEM((fronts, inner_rows, columns), jnp.float32),
            pltpu.SemaphoreType.DMA((fronts, blocks)),
            pltpu.SemaphoreType.DMA((2, fronts, outer)),
            pltpu.SemaphoreType.DMA((fronts, outer)),
            pltpu.SemaphoreType.DMA((4,)),
            pltpu.SemaphoreType.DMA((2, fronts)),
        ],
        compiler_params=pltpu.CompilerParams(
            collective_id=0, has_side_effects=True, vmem_limit_bytes=48 * 1024 * 1024
        ),
    )(incident, green_interior, green_next, sources)


def solution(mesh):
    return jax.shard_map(
        functools.partial(local, mesh.shape["slab"], mesh.shape["trace"]),
        mesh=mesh,
        in_specs=(
            P(None, "trace", None),
            P("slab", None, "trace", None),
            P("slab", None, "trace", None),
            P("slab", None, "trace", None),
        ),
        out_specs=(P("slab", None, "trace", None), P("slab", None, "trace", None)),
        check_vma=False,
    )
```

```python
import functools

import jax
import jax.numpy as jnp
from jax import lax
from jax.experimental import pallas as pl
from jax.experimental.pallas import tpu as pltpu
from jax.sharding import PartitionSpec as P

MESH = pl.DeviceIdType.MESH
INNER = 2


def chunk_count(blocks, rows):
    count = 4
    while count > 1 and (blocks % (count * INNER) or (blocks // count * rows) % 128):
        count //= 2
    return count


def flip(value, mask):
    result = value
    bit = 1
    while bit <= mask:
        if mask & bit:
            result = result + bit - 2 * bit * lax.rem(result // bit, 2)
        bit *= 2
    return result


def visit_order(count):
    return [0] + list(range(count - 1, 0, -1))


def combine(first, second):
    lane = lax.broadcasted_iota(jnp.int32, first.shape, 1)
    half = first.shape[1] // 2
    turned = pltpu.roll(second, half, 1)
    return first + jnp.where(lane < half, -turned, turned)


def kernel(
    slabs,
    blocks,
    incident,
    green_interior,
    green_next,
    sources,
    interior,
    traces,
    entering,
    leaving,
    first_out,
    next_op,
    inner_op,
    incoming,
    own_sources,
    next_sum,
    inner_sum,
    trace_out,
    inner_out,
    recv_sem,
    direct_sem,
    relay_sem,
    load_sem,
    store_sem,
):
    fronts, _, rows, columns = entering.shape
    inner_rows = inner_op.shape[1]
    depth = next_op.shape[2]
    outer = blocks // INNER
    chunks = chunk_count(blocks, rows)
    per_chunk = blocks // chunks
    width = depth // chunks
    slab = lax.axis_index("slab")
    me = lax.axis_index("trace")
    lane_pos = lax.rem(me, INNER)
    my_outer = me // INNER
    partner = me + 1 - 2 * lane_pos
    first_slab = slab == 0
    last_slab = slab == slabs - 1
    my_chunk = me // per_chunk

    def load_incident(front):
        return pltpu.make_async_copy(
            incident.at[front], incoming.at[front], load_sem.at[3 + front]
        )

    load_next = pltpu.make_async_copy(green_next.at[0], next_op, load_sem.at[0])
    load_sources = pltpu.make_async_copy(sources.at[0], own_sources, load_sem.at[1])
    load_inner = pltpu.make_async_copy(green_interior.at[0], inner_op, load_sem.at[2])

    @pl.when(first_slab | last_slab)
    def _():
        for front in range(fronts):
            load_incident(front).start()

    load_next.start()
    load_sources.start()
    load_inner.start()

    barrier = pltpu.get_barrier_semaphore()

    def greet(target_slab, target):
        pl.semaphore_signal(
            barrier, inc=1, device_id={"slab": target_slab, "trace": target}, device_id_type=MESH
        )

    def row_peer(step):
        return flip(my_outer, step) * INNER + lane_pos

    greet(slab, partner)

    @pl.when(first_slab)
    def _():
        for step in range(1, outer):
            greet(slabs - 1, row_peer(step))

    @pl.when(jnp.logical_not(first_slab))
    def _():
        for step in range(outer):
            greet(slab - 1, row_peer(step))

    peers = jnp.where(last_slab, outer, outer + 1)
    pl.semaphore_wait(barrier, peers)

    def first_copy(front, step):
        return pltpu.make_async_remote_copy(
            src_ref=first_out.at[front],
            dst_ref=entering.at[front, me],
            send_sem=direct_sem.at[front, step],
            recv_sem=recv_sem.at[front, me],
            device_id={"slab": 0, "trace": row_peer(step)},
            device_id_type=MESH,
        )

    def next_copy(front, step):
        return pltpu.make_async_remote_copy(
            src_ref=leaving.at[front],
            dst_ref=entering.at[front, me],
            send_sem=direct_sem.at[front, step],
            recv_sem=recv_sem.at[front, me],
            device_id={"slab": slab + 1, "trace": row_peer(step)},
            device_id_type=MESH,
        )

    def relay_copy(front, block):
        return pltpu.make_async_remote_copy(
            src_ref=entering.at[front, block],
            dst_ref=entering.at[front, block],
            send_sem=relay_sem.at[front, block // INNER],
            recv_sem=recv_sem.at[front, block],
            device_id={"slab": slab, "trace": partner},
            device_id_type=MESH,
        )

    def store_trace(front):
        return pltpu.make_async_copy(
            trace_out.at[front], traces.at[0, front], store_sem.at[0, front]
        )

    def store_inner(front):
        return pltpu.make_async_copy(
            inner_out.at[front], interior.at[0, front], store_sem.at[1, front]
        )

    @pl.when(first_slab)
    def _():
        for front in range(fronts):
            load_incident(front).wait()
            entering[front, me] = incoming[front].astype(jnp.bfloat16)

    @pl.when(last_slab)
    def _():
        for front in range(fronts):
            load_incident(front).wait()
            first_out[front] = incoming[front].astype(jnp.bfloat16)
            for step in visit_order(outer)[1:]:
                first_copy(front, step).start()

    def chunk_at(order):
        return flip(my_chunk, visit_order(chunks)[order])

    def vectors(front, chunk):
        return entering[front, pl.ds(chunk * per_chunk, per_chunk)].reshape(width, columns)

    def add_chunk(op, total, front, chunk, fresh):
        start = pl.multiple_of(chunk * width, width)
        halves = op.shape[1]
        matrix = op[:, :, pl.ds(start, width)].reshape(2 * halves, width)
        product = jnp.dot(
            matrix, vectors(front, chunk), preferred_element_type=jnp.float32
        )
        if fresh:
            total[...] = product
        else:
            total[...] += product

    def inner_chunk(front, order):
        add_chunk(inner_op, inner_sum, front, chunk_at(order), order == 0)
        if order == chunks - 1:
            inner_out[front] = combine(inner_sum[0:inner_rows], inner_sum[inner_rows:])
            store_inner(front).start()

    def one_front(front, carry):
        for order in range(chunks):
            for index in range(per_chunk // INNER):
                block = chunk_at(order) * per_chunk + index * INNER + lane_pos

                @pl.when(jnp.logical_not(first_slab & (block == me)))
                def _():
                    relay_copy(front, block).wait_recv()

                relay_copy(front, block).start()

            @pl.when(front > 0)
            def _():
                inner_chunk(front - 1, order)

        @pl.when(front == 0)
        def _():
            load_next.wait()
            load_sources.wait()
            load_inner.wait()

        for order in range(chunks):
            for index in range(per_chunk // INNER):
                block = chunk_at(order) * per_chunk + index * INNER + 1 - lane_pos
                relay_copy(front, block).wait_recv()
            add_chunk(next_op, next_sum, front, chunk_at(order), order == 0)

        result = combine(next_sum[0:rows], next_sum[rows:]) + own_sources[front]
        trace_out[front] = result
        leaving[front] = result.astype(jnp.bfloat16)

        @pl.when(jnp.logical_not(last_slab))
        def _():
            for step in visit_order(outer):
                next_copy(front, step).start()

        store_trace(front).start()
        return carry

    lax.fori_loop(0, fronts, one_front, 0)
    for order in range(chunks):
        inner_chunk(fronts - 1, order)

    def drain(front, carry):
        @pl.when(last_slab)
        def _():
            for step in range(1, outer):
                first_copy(front, step).wait_send()

        @pl.when(jnp.logical_not(last_slab))
        def _():
            for step in range(outer):
                next_copy(front, step).wait_send()

        for index in range(outer):
            relay_copy(front, index * INNER + lane_pos).wait_send()
        store_trace(front).wait()
        store_inner(front).wait()
        return carry

    lax.fori_loop(0, fronts, drain, 0)


def local(slabs, blocks, incident, green_interior, green_next, sources):
    fronts, rows, columns = incident.shape
    inner_rows = green_interior.shape[2]
    depth = green_next.shape[3]
    outer = blocks // INNER
    in_hbm = pl.BlockSpec(memory_space=pltpu.HBM)
    anywhere = pl.BlockSpec(memory_space=pl.ANY)
    return pl.pallas_call(
        functools.partial(kernel, slabs, blocks),
        out_shape=(
            jax.ShapeDtypeStruct((1, fronts, inner_rows, columns), jnp.float32),
            jax.ShapeDtypeStruct((1, fronts, rows, columns), jnp.float32),
        ),
        in_specs=[in_hbm] * 4,
        out_specs=(anywhere, anywhere),
        scratch_shapes=[
            pltpu.VMEM((fronts, blocks, rows, columns), jnp.bfloat16),
            pltpu.VMEM((fronts, rows, columns), jnp.bfloat16),
            pltpu.VMEM((fronts, rows, columns), jnp.bfloat16),
            pltpu.VMEM((2, rows, depth), jnp.bfloat16),
            pltpu.VMEM((2, inner_rows, depth), jnp.bfloat16),
            pltpu.VMEM((fronts, rows, columns), jnp.float32),
            pltpu.VMEM((fronts, rows, columns), jnp.float32),
            pltpu.VMEM((2 * rows, columns), jnp.float32),
            pltpu.VMEM((2 * inner_rows, columns), jnp.float32),
            pltpu.VMEM((fronts, rows, columns), jnp.float32),
            pltpu.VMEM((fronts, inner_rows, columns), jnp.float32),
            pltpu.SemaphoreType.DMA((fronts, blocks)),
            pltpu.SemaphoreType.DMA((fronts, outer)),
            pltpu.SemaphoreType.DMA((fronts, outer)),
            pltpu.SemaphoreType.DMA((3 + fronts,)),
            pltpu.SemaphoreType.DMA((2, fronts)),
        ],
        compiler_params=pltpu.CompilerParams(
            collective_id=0, has_side_effects=True, vmem_limit_bytes=48 * 1024 * 1024
        ),
    )(incident, green_interior, green_next, sources)


def solution(mesh):
    return jax.shard_map(
        functools.partial(local, mesh.shape["slab"], mesh.shape["trace"]),
        mesh=mesh,
        in_specs=(
            P(None, "trace", None),
            P("slab", None, "trace", None),
            P("slab", None, "trace", None),
            P("slab", None, "trace", None),
        ),
        out_specs=(P("slab", None, "trace", None), P("slab", None, "trace", None)),
        check_vma=False,
    )
```
